512 devices in a mesh: tm: 32 (over z, core), row: 16 (over x, y).
Axes of the slice: x: 4, y: 4, z: 16, core: 2. Of those that a mesh axis runs over, the one named last changes fastest.
Arguments:
- video: bfloat16 [32, 4, 384, 1024], P('tm', None, 'row'), may hold values from -6 to 6
- stem_weight: bfloat16 [64, 4, 3, 3], replicated, may hold values from -1 to 1
- w_qkv: bfloat16 [1536, 2304], P('tm'), may hold values from -0.15625 to 0.15625
- decay: float32 [32, 6], P('tm'), may hold values from 0.04 to 1, as said below
Outputs:
- mixed: bfloat16 [32, 32, 128, 768], P('tm', 'row')
The draws below stay inside these ranges and needn't reach their ends.
Inputs may be any that keep to these rules, and one draw needn't show every extreme that they name: decay lies in (0, 1].
All inputs are finite; a program needn't handle non-finite values.
Results may differ from the reference program's by a relative error of at most 0.012.
Values may be sent and summed in bfloat16 or wider, within the bound.
A program may use at most 128 MiB of HBM per device.

```python
import jax
import jax.numpy as jnp
from jax import lax

FIELDS = 4
CH = 64
HEADS = 6
DH = 128
W = 1024
D = 1536
HD = 768
WINDOW_FRAMES = 32
ROWS = 384
PROWS = 32
PCOLS = 128


def draw_decay(key, part):
    stacked_keys = jax.random.split(key, 6)
    picked = jax.random.randint(stacked_keys[0], (HEADS,), 0, 8)
    fast_heads = picked < 4
    fast_rate = jax.random.uniform(stacked_keys[1], (HEADS,), jnp.float32, 0.2, 0.5)
    slow_speed = jax.random.uniform(stacked_keys[2], (HEADS,), jnp.float32, 0.2, 1.0)
    slow_rate = jnp.exp(-slow_speed / WINDOW_FRAMES)
    base_rate = jnp.where(fast_heads, fast_rate, slow_rate)
    jitter = jax.random.uniform(stacked_keys[3], (WINDOW_FRAMES, HEADS), jnp.float32, 0.5, 1.5)
    decay_rates = base_rate[None, :] ** jitter
    token_group = jax.random.randint(stacked_keys[4], (WINDOW_FRAMES, 1), 0, WINDOW_FRAMES) < 3
    group_boundary = jax.random.uniform(stacked_keys[5], (WINDOW_FRAMES, 1), jnp.float32, 0.5, 0.8)
    return jnp.where(token_group, decay_rates * group_boundary, decay_rates).astype(jnp.float32)


def steps_of(stream_key, extent, cuts, low, top_value):
    def one(dim, parts):
        heights = jax.random.uniform(jax.random.fold_in(jax.random.fold_in(stream_key, 6), dim), (parts,), jnp.float32, low / len(cuts), top_value / len(cuts))
        return jnp.repeat(jnp.exp(heights), extent[dim] // parts).reshape((-1,) + (1,) * (len(extent) - dim - 1))

    loudness = one(*cuts[0])
    for cut in cuts[1:]:
        loudness = loudness * one(*cut)
    return loudness


def normal_values(key, shape, spread, bound, cuts=(), held_as=jnp.bfloat16):
    result = jax.random.normal(key, shape, jnp.float32) * spread
    if len(cuts) > 0:
        result = steps_of(key, shape, cuts, -0.22, 0.18) * result
    return jnp.clip(result, min=-bound, max=bound).astype(held_as)


def setup_inputs(seed: int = 0) -> dict:
    key_of = jax.random.split(jax.random.key(seed), 5)
    video = normal_values(key_of[0], (WINDOW_FRAMES, FIELDS, ROWS, W), 1.0, 6.0, ((0, 32), (2, 16)))
    stem_weight = normal_values(key_of[1], (CH, FIELDS, 3, 3), (FIELDS * 9) ** -0.5, 1.0)
    w_qkv = normal_values(key_of[2], (D, 3 * HD), D ** -0.5, 0.15625, ((0, 32),))
    decay = draw_decay(jax.random.fold_in(key_of[4], 71), 0)
    return {"video": video, "stem_weight": stem_weight, "w_qkv": w_qkv, "decay": decay}


def patch_tokens(frame_data, stem_weight):
    padded = jnp.pad(frame_data, ((0, 0), (1, 0), (1, 0)))
    stem_out = lax.conv_general_dilated(padded[None], stem_weight, (2, 2), 'VALID', dimension_numbers=('NCHW', 'OIHW', 'NCHW'), preferred_element_type=jnp.float32)[0]
    features = jnp.tanh(stem_out).astype(jnp.bfloat16)
    channels = features.shape[0]
    patch_rows = features.shape[1] // 6
    patch_cols = features.shape[2] // 4
    shaped = features.reshape(channels, patch_rows, 6, patch_cols, 4).transpose(1, 3, 0, 2, 4)
    return shaped.reshape(patch_rows * patch_cols, channels * 24)

def reference(video, stem_weight, w_qkv, decay):

    def advance(carry_state, inputs):
        frame_data, frame_rate = inputs
        frame_tokens = patch_tokens(frame_data, stem_weight)
        token_count = frame_tokens.shape[0]
        projected = jnp.dot(frame_tokens, w_qkv, preferred_element_type=jnp.float32).astype(jnp.bfloat16)
        queries = projected[:, :HD].reshape(token_count, HEADS, DH).astype(jnp.float32)
        keys = projected[:, HD:2 * HD].reshape(token_count, HEADS, DH).astype(jnp.float32)
        values = projected[:, 2 * HD:].reshape(token_count, HEADS, DH).astype(jnp.float32)
        outer_sum = jnp.einsum('nhd,nhe->hde', keys, values)
        carry_state = frame_rate[:, None, None] * carry_state + outer_sum
        state_bf = carry_state.astype(jnp.bfloat16).astype(jnp.float32)
        attended = jnp.einsum('nhd,hde->nhe', queries, state_bf)
        attended = attended * lax.rsqrt(lax.optimization_barrier(jnp.mean(attended * attended, axis=-1, keepdims=True)) + 1e-06)
        return (carry_state, attended.reshape(PROWS, PCOLS, HD).astype(jnp.bfloat16))
    initial = jnp.zeros((HEADS, DH, DH), jnp.float32)
    final_state, mixed = lax.scan(advance, initial, (video, decay))
    return mixed
```

```python
import jax
import jax.numpy as jnp
from jax import lax
from jax.experimental import pallas as pl
from jax.experimental.pallas import tpu as pltpu
from jax.sharding import PartitionSpec as P

HEADS = 6
DH = 128
ROW = 16
QUAD = 8
GROUPS = 4
SHARE = HEADS * DH // ROW
MESH = pl.DeviceIdType.MESH


def shifted(block, axis, distance):
    devices = range(lax.axis_size(axis))
    route = [(i - distance, i) for i in devices if i - distance in devices]
    return lax.ppermute(block, axis, route)


def copy_to(src, dst, sems, slot, axis, index):
    return pltpu.make_async_remote_copy(
        src_ref=src,
        dst_ref=dst,
        send_sem=sems.at[0, slot],
        recv_sem=sems.at[1, slot],
        device_id={axis: index},
        device_id_type=MESH,
    )


def attend_kernel(
    proj_ref,
    decay_ref,
    out_ref,
    kv_buf,
    part_buf,
    kv_share,
    quad_kv,
    quad_decay,
    total,
    total_decay,
    group_kv,
    group_decay,
    state_share,
    state_buf,
    row_sems,
    quad_sems,
    rate_sems,
    group_sems,
    product_sems,
    state_sems,
):
    tm = lax.axis_index("tm")
    row = lax.axis_index("row")
    group = tm // QUAD
    seat = lax.rem(tm, QUAD)
    first = group * QUAD

    row_peers = [lax.rem(row + d, ROW) for d in range(1, ROW)]
    quad_peers = [first + lax.rem(seat + d, QUAD) for d in range(1, QUAD)]
    group_peers = [lax.rem(tm + d * QUAD, QUAD * GROUPS) for d in range(1, GROUPS)]

    barrier = pltpu.get_barrier_semaphore()
    for peer in row_peers:
        pl.semaphore_signal(barrier, inc=1, device_id={"row": peer}, device_id_type=MESH)
    for peer in quad_peers + group_peers:
        pl.semaphore_signal(barrier, inc=1, device_id={"tm": peer}, device_id_type=MESH)

    width = HEADS * DH
    for h in range(HEADS):
        keys = proj_ref[:, width + h * DH : width + (h + 1) * DH]
        values = proj_ref[:, 2 * width + h * DH : 2 * width + (h + 1) * DH]
        outer = lax.dot_general(
            keys, values, (((0,), (0,)), ((), ())), preferred_element_type=jnp.float32
        )
        kv_buf[h * DH : (h + 1) * DH, :] = outer.astype(jnp.bfloat16)

    pl.semaphore_wait(barrier, ROW + QUAD + GROUPS - 3)

    def share_of(index):
        return kv_buf.at[pl.ds(pl.multiple_of(index * SHARE, 16), SHARE), :]

    sends = []
    for d in range(1, ROW):
        copy = copy_to(share_of(row_peers[d - 1]), part_buf.at[d], row_sems, d, "row", row_peers[d - 1])
        copy.start()
        sends.append(copy)
    rates = []
    for d in range(1, QUAD):
        copy = copy_to(decay_ref, quad_decay.at[d], rate_sems, d, "tm", quad_peers[d - 1])
        copy.start()
        rates.append(copy)
    quad_decay[0] = decay_ref[...]

    start = row * SHARE
    summed = kv_buf[pl.ds(pl.multiple_of(start, 16), SHARE), :].astype(jnp.float32)
    for copy in rates:
        copy.wait()

    def decay_of(offset):
        return quad_decay[offset]

    product = jnp.ones((8, 128), jnp.float32)
    for i in range(QUAD):
        product = product * quad_decay[i]
    total_decay[...] = product

    for d in range(1, ROW):
        sends[d - 1].wait()
        summed = summed + part_buf[d].astype(jnp.float32)
    kv_share[...] = summed.astype(jnp.bfloat16)

    quads = []
    for d in range(1, QUAD):
        copy = copy_to(kv_share, quad_kv.at[d], quad_sems, d, "tm", quad_peers[d - 1])
        copy.start()
        quads.append(copy)
    products = []
    for d in range(1, GROUPS):
        copy = copy_to(
            total_decay, group_decay.at[d], product_sems, d, "tm", group_peers[d - 1]
        )
        copy.start()
        products.append(copy)

    head = (start + lax.broadcasted_iota(jnp.int32, (SHARE, DH), 0)) // DH

    def expand(tile):
        factor = jnp.zeros((SHARE, DH), jnp.float32)
        for h in range(HEADS):
            factor = jnp.where(head == h, tile[h : h + 1, :], factor)
        return factor

    quad_kv[0] = kv_share[...]
    for copy in quads:
        copy.wait()

    def pass_one(i, running):
        slot = lax.rem(seat - i + QUAD, QUAD)
        return expand(quad_decay[slot]) * running + quad_kv[slot].astype(jnp.float32)

    whole = lax.fori_loop(0, QUAD, pass_one, jnp.zeros((SHARE, DH), jnp.float32))
    total[...] = whole.astype(jnp.bfloat16)

    groups = []
    for d in range(1, GROUPS):
        copy = copy_to(total, group_kv.at[d], group_sems, d, "tm", group_peers[d - 1])
        copy.start()
        groups.append(copy)
    for copy in products:
        copy.wait()
    for copy in groups:
        copy.wait()

    def pass_groups(g, running):
        slot = lax.rem(group - g + GROUPS, GROUPS)
        return expand(group_decay[slot]) * running + group_kv[slot].astype(jnp.float32)

    running = lax.fori_loop(0, group, pass_groups, jnp.zeros((SHARE, DH), jnp.float32))
    running = lax.fori_loop(0, seat + 1, pass_one, running)
    state_share[...] = running.astype(jnp.bfloat16)

    states = []
    for d in range(1, ROW):
        copy = copy_to(
            state_share, state_buf.at[row], state_sems, d, "row", row_peers[d - 1]
        )
        copy.start()
        states.append(copy)
    state_buf[row] = state_share[...]
    for copy in states:
        copy.wait_send()
    for d in range(1, ROW):
        sender = lax.rem(row - d + ROW, ROW)
        copy_to(state_share, state_buf.at[sender], state_sems, d, "row", sender).wait_recv()

    state = state_buf[...].reshape(HEADS * DH, DH)
    for h in range(HEADS):
        queries = proj_ref[:, h * DH : (h + 1) * DH]
        attended = jnp.dot(
            queries, state[h * DH : (h + 1) * DH, :], preferred_element_type=jnp.float32
        )
        scale = lax.rsqrt(jnp.mean(attended * attended, axis=-1, keepdims=True) + 1e-06)
        out_ref[:, h * DH : (h + 1) * DH] = (attended * scale).astype(jnp.bfloat16)


def attend(projected, decay_tile):
    tokens = projected.shape[0]
    bf, f32 = jnp.bfloat16, jnp.float32
    return pl.pallas_call(
        attend_kernel,
        out_shape=jax.ShapeDtypeStruct((tokens, HEADS * DH), bf),
        in_specs=[pl.BlockSpec(memory_space=pltpu.VMEM)] * 2,
        out_specs=pl.BlockSpec(memory_space=pltpu.VMEM),
        scratch_shapes=[
            pltpu.VMEM((HEADS * DH, DH), bf),
            pltpu.VMEM((ROW, SHARE, DH), bf),
            pltpu.VMEM((SHARE, DH), bf),
            pltpu.VMEM((QUAD, SHARE, DH), bf),
            pltpu.VMEM((QUAD, 8, 128), f32),
            pltpu.VMEM((SHARE, DH), bf),
            pltpu.VMEM((8, 128), f32),
            pltpu.VMEM((GROUPS, SHARE, DH), bf),
            pltpu.VMEM((GROUPS, 8, 128), f32),
            pltpu.VMEM((SHARE, DH), bf),
            pltpu.VMEM((ROW, SHARE, DH), bf),
            pltpu.SemaphoreType.DMA((2, ROW)),
            pltpu.SemaphoreType.DMA((2, QUAD)),
            pltpu.SemaphoreType.DMA((2, QUAD)),
            pltpu.SemaphoreType.DMA((2, GROUPS)),
            pltpu.SemaphoreType.DMA((2, GROUPS)),
            pltpu.SemaphoreType.DMA((2, ROW)),
        ],
        compiler_params=pltpu.CompilerParams(collective_id=0, has_side_effects=True),
        name="attend",
    )(projected, decay_tile)


def local(video, stem_weight, w_qkv, decay):
    frames_dev = video.shape[0]
    row = lax.axis_index("row")
    depth = w_qkv.shape[0] // ROW
    piece = lax.dynamic_slice_in_dim(w_qkv, row * depth, depth, axis=0)
    weights = lax.all_gather(piece, ("tm", "row"), axis=0, tiled=True)

    upper_row = shifted(video[:, :, -1:, :], "row", 1)
    padded = jnp.concatenate([upper_row, video], axis=2)
    padded = jnp.pad(padded, ((0, 0), (0, 0), (0, 0), (1, 0)))
    stem_out = lax.conv_general_dilated(
        padded,
        stem_weight,
        (2, 2),
        "VALID",
        dimension_numbers=("NCHW", "OIHW", "NCHW"),
        preferred_element_type=jnp.float32,
    )
    features = jnp.tanh(stem_out).astype(jnp.bfloat16)
    channels = features.shape[1]
    patch_rows = features.shape[2] // 6
    patch_cols = features.shape[3] // 4
    shaped = features.reshape(frames_dev, channels, patch_rows, 6, patch_cols, 4).transpose(
        0, 2, 4, 1, 3, 5
    )
    tokens = shaped.reshape(frames_dev * patch_rows * patch_cols, channels * 24)
    projected = jnp.dot(tokens, weights, preferred_element_type=jnp.float32).astype(jnp.bfloat16)
    decay_tile = jnp.pad(jnp.broadcast_to(decay.reshape(HEADS, 1), (HEADS, 128)), ((0, 2), (0, 0)))
    mixed = attend(projected, decay_tile)
    return mixed.reshape(frames_dev, patch_rows, patch_cols, HEADS * DH)


def solution(mesh):
    return jax.shard_map(
        local,
        mesh=mesh,
        in_specs=(P("tm", None, "row", None), P(), P("tm", None), P("tm", None)),
        out_specs=P("tm", "row", None, None),
        check_vma=False,
    )
```

```python
import jax
import jax.numpy as jnp
from jax import lax
from jax.experimental import pallas as pl
from jax.experimental.pallas import tpu as pltpu
from jax.sharding import PartitionSpec as P

HEADS = 6
HALF = 3
DH = 128
ROW = 16
SIDE = 4
ZS = 16
SHARE = 24
WIDE = HALF * DH
COLS = 3 * WIDE
DEPTH = 48
MESH = pl.DeviceIdType.MESH
BF = jnp.bfloat16
F32 = jnp.float32


def remote(src, dst, send, recv, where):
    return pltpu.make_async_remote_copy(
        src_ref=src,
        dst_ref=dst,
        send_sem=send,
        recv_sem=recv,
        device_id=where,
        device_id_type=MESH,
    )


def one_hot(rows, columns, target, axis):
    places = lax.broadcasted_iota(jnp.int32, (rows, columns), axis)
    return jnp.where(places == target, 1.0, 0.0).astype(BF)


def kernel(
    video_ref,
    last_ref,
    w_ref,
    stem_ref,
    decay_ref,
    out_ref,
    images,
    wbuf,
    spread,
    stem,
    tokens,
    projected,
    rates,
    pair_rate,
    kv_buf,
    parts,
    pair_kv,
    scan_kv,
    scan_rate,
    state_share,
    state_buf,
    mixed_out,
    mixed_in,
    near_sems,
    main_send,
    main_recv,
    last_send,
    last_recv,
    own_sems,
    pass_sems,
    swap_sems,
    row_sems,
    rate_sems,
    scan_sems,
    state_sems,
):
    tm = lax.axis_index("tm")
    row = lax.axis_index("row")
    z, c = tm // 2, lax.rem(tm, 2)
    x, y = row // SIDE, lax.rem(row, SIDE)
    sibling = tm + 1 - 2 * c
    other = 1 - c
    below = lax.rem(row + 1, ROW)
    above = lax.rem(row + ROW - 1, ROW)
    parity = lax.rem(row, 2)
    block = row // 2
    last_parity = lax.rem(x, 2)

    barrier = pltpu.get_barrier_semaphore()

    def greet(where):
        pl.semaphore_signal(barrier, inc=1, device_id=where, device_id_type=MESH)

    def later_z(d):
        return lax.rem(z + d, ZS)

    def earlier_z(d):
        return lax.rem(z - d + ZS, ZS)

    for d in range(ZS):
        for t in range(2):
            if d > 0:
                greet({"tm": 2 * later_z(d) + t})
    greet({"tm": sibling})
    for d in range(1, ROW):
        greet({"row": lax.rem(row + d, ROW)})
    greet({"tm": sibling, "row": below})
    greet({"tm": sibling, "row": above})

    def source(b, t):
        part = b // HALF
        start = part * HEADS * DH + t * WIDE + (b - part * HALF) * DH
        return w_ref.at[:, pl.ds(pl.multiple_of(start, DH), DH)]

    def place(zi, ci, b):
        return wbuf.at[zi, ci, :, pl.ds(pl.multiple_of(b * DH, DH), DH)]

    pl.semaphore_wait(barrier, 2 * ZS - 1 + ROW - 1 + 2)

    near = [
        remote(video_ref, images.at[c, 0:96], near_sems.at[0, 0], near_sems.at[1, 0], {"tm": sibling}),
        remote(last_ref, images.at[c, 96:112], near_sems.at[0, 1], near_sems.at[1, 1], {"row": below}),
        remote(
            last_ref,
            images.at[c, 96:112],
            near_sems.at[0, 2],
            near_sems.at[1, 2],
            {"tm": sibling, "row": below},
        ),
        remote(decay_ref, rates.at[c], near_sems.at[0, 3], near_sems.at[1, 3], {"tm": sibling}),
    ]
    for copy in near:
        copy.start()

    def scatter(b, send, recv):
        copies = []
        for d in range(1, ZS):
            for t in range(2):
                copies.append(
                    remote(
                        source(b, t),
                        place(z, c, b),
                        send.at[t, d],
                        recv.at[d],
                        {"tm": 2 * later_z(d) + t},
                    )
                )
        copies.append(
            remote(source(b, other), place(z, c, b), send.at[0, 0], recv.at[0], {"tm": sibling})
        )
        return copies

    def arrived(b, ci, recv, zi):
        d = lax.rem(z - zi + ZS, ZS)

        @pl.when(jnp.logical_or(d != 0, c != ci))
        def _():
            remote(source(b, 0), place(zi, ci, b), recv.at[d], recv.at[d], {"tm": sibling}).wait_recv()

    last_block = 8

    @pl.when(c == parity)
    def _():
        for copy in scatter(block, main_send, main_recv):
            copy.start()
        wbuf[z, c, :, pl.ds(pl.multiple_of(block * DH, DH), DH)] = source(block, c)[...]

    @pl.when(c == last_parity)
    def _():
        for copy in scatter(last_block, last_send, last_recv):
            copy.start()
        wbuf[z, c, :, last_block * DH : (last_block + 1) * DH] = source(last_block, c)[...]

    images[c, 0:96, :] = video_ref[...]
    rates[c] = decay_ref[...]
    copies_of = lax.broadcasted_iota(jnp.int32, (1, 1536), 1)
    channel = copies_of // 24
    position = copies_of - channel * 24
    repeat = one_hot(64, 1536, channel, 0)
    kernels = jnp.dot(stem_ref[...], repeat, preferred_element_type=F32)
    for ij in range(24):
        spread[ij * 48 : (ij + 1) * 48, :] = jnp.where(position == ij, kernels, 0.0).astype(BF)
    term = lax.broadcasted_iota(jnp.int32, (1, 1152), 1)
    ij = term // 48
    fab = term - ij * 48
    i, j = ij // 4, ij - (ij // 4) * 4
    f = fab // 9
    a = (fab - f * 9) // 3
    b = fab - f * 9 - a * 3
    goal = jnp.where(fab < 36, (2 * j + b) * 64 + f * 16 + 2 * i + a, -1)
    chosen = one_hot(576, 1152, goal, 0)
    for n in range(3):
        stem[:, n * 512 : (n + 1) * 512] = jnp.dot(
            chosen, spread[:, n * 512 : (n + 1) * 512], preferred_element_type=F32
        ).astype(BF)

    for copy in near:
        copy.wait()

    line = lax.broadcasted_iota(jnp.int32, (128, 1), 0)
    patch, field, tap = line // 64, lax.rem(line, 64) // 16, lax.rem(line, 16)
    image_row = 12 * patch - 1 + tap
    above_row = jnp.where(row == 0, -1, 96 + field)
    picked = jnp.where(image_row < 0, above_row, field * 24 + image_row)
    picked = jnp.where(tap > 12, -1, picked)
    row_pick = one_hot(128, 112, picked, 1)
    column = lax.broadcasted_iota(jnp.int32, (1, 1152), 1)
    tap_column = 8 * lax.rem(column, 128) - 1 + column // 128
    column_pick = one_hot(1024, 1152, tap_column, 0)
    pair_rate[...] = rates[0] * rates[1]
    for frame in range(2):
        rows_of = jnp.dot(row_pick, images[frame], preferred_element_type=F32).astype(BF)
        taps = jnp.dot(rows_of, column_pick, preferred_element_type=F32).astype(BF)
        for p in range(2):
            stacked = jnp.concatenate(
                [taps[p * 64 : (p + 1) * 64, k * 128 : (k + 1) * 128] for k in range(9)], axis=0
            )
            at = (frame * 2 + p) * 128
            for n in range(3):
                made = lax.dot_general(
                    stacked,
                    stem[:, n * 512 : (n + 1) * 512],
                    (((0,), (0,)), ((), ())),
                    preferred_element_type=F32,
                )
                tokens[at : at + 128, n * 512 : (n + 1) * 512] = jnp.tanh(made).astype(BF)

    def piece(quad, chip, start, count):
        return wbuf.at[
            pl.ds(quad * 4 + start, count),
            lax.rem(chip, 2),
            :,
            pl.ds(pl.multiple_of((chip // 2) * DH, DH), DH),
        ]

    def chip_at(dx, dy):
        return lax.rem(x + dx + SIDE, SIDE) * SIDE + lax.rem(y + dy + SIDE, SIDE)

    def step(axis, d):
        return chip_at(d, 0) if axis == 0 else chip_at(0, d)

    sent = []

    def send_own(k):
        quad = lax.rem(z // 4 + k, 4)
        for o in range(4):
            arrived(block, parity, main_recv, quad * 4 + o)
        for d in range(1, SIDE):
            for axis in range(2):
                copy = remote(
                    piece(quad, row, 0, 4),
                    piece(quad, row, 0, 4),
                    own_sems.at[0, k, axis, d],
                    own_sems.at[1, k, axis, d],
                    {"row": step(axis, d)},
                )
                copy.start()
                sent.append(copy)

    def pass_on(k):
        quad = lax.rem(z // 4 + k, 4)
        for e in range(1, SIDE):
            for axis in range(2):
                origin = step(axis, -e)
                here = piece(quad, origin, 0, 4)
                remote(
                    here, here, own_sems.at[0, k, axis, e], own_sems.at[1, k, axis, e], {"row": origin}
                ).wait_recv()
                half = piece(quad, origin, 2 * axis, 2)
                for d in range(1, SIDE):
                    copy = remote(
                        half,
                        half,
                        pass_sems.at[0, k, axis, d, e],
                        pass_sems.at[1, k, axis, d, e],
                        {"row": step(1 - axis, d)},
                    )
                    copy.start()
                    sent.append(copy)

    send_own(0)
    for k in range(1, 4):
        send_own(k)
        pass_on(k - 1)
    pass_on(3)

    for zi in range(ZS):
        arrived(last_block, last_parity, last_recv, zi)
    mine = wbuf.at[:, last_parity, :, last_block * DH : (last_block + 1) * DH]
    neighbour = (x + 1 - 2 * last_parity) * SIDE + y
    swap = remote(mine, mine, swap_sems.at[0], swap_sems.at[1], {"row": neighbour})
    swap.start()

    for k in range(4):
        quad = lax.rem(z // 4 + k, 4)
        for axis in range(2):
            for d in range(1, SIDE):
                for e in range(1, SIDE):
                    origin = chip_at(-e, -d) if axis == 0 else chip_at(-d, -e)
                    half = piece(quad, origin, 2 * axis, 2)
                    remote(
                        half,
                        half,
                        pass_sems.at[0, k, axis, d, e],
                        pass_sems.at[1, k, axis, d, e],
                        {"row": origin},
                    ).wait_recv()
    swap.wait_send()
    theirs = wbuf.at[:, 1 - last_parity, :, last_block * DH : (last_block + 1) * DH]
    remote(theirs, theirs, swap_sems.at[0], swap_sems.at[1], {"row": neighbour}).wait_recv()
    for copy in sent:
        copy.wait_send()

    def project(part):
        weights = wbuf[:, :, :, part * WIDE : (part + 1) * WIDE].reshape(1536, WIDE)
        projected[:, part * WIDE : (part + 1) * WIDE] = jnp.dot(
            tokens[...], weights, preferred_element_type=F32
        ).astype(BF)

    project(1)
    project(2)

    sums = []
    for frame in range(2):
        heads = []
        for h in range(HALF):
            keys = projected[frame * 256 : (frame + 1) * 256, WIDE + h * DH : WIDE + (h + 1) * DH]
            values = projected[
                frame * 256 : (frame + 1) * 256, 2 * WIDE + h * DH : 2 * WIDE + (h + 1) * DH
            ]
            heads.append(
                lax.dot_general(
                    keys, values, (((0,), (0,)), ((), ())), preferred_element_type=F32
                )
            )
        sums.append(jnp.concatenate(heads, axis=0).reshape(ROW, SHARE, DH))
    kv_buf[...] = jnp.concatenate(sums, axis=1).astype(BF)

    reduces = []
    for d in range(1, ROW):
        peer = lax.rem(row + d, ROW)
        copy = remote(
            kv_buf.at[peer], parts.at[d], row_sems.at[0, d], row_sems.at[1, d], {"row": peer}
        )
        copy.start()
        reduces.append(copy)
    rate_copies = []
    for d in range(1, ZS):
        copy = remote(
            pair_rate,
            scan_rate.at[d],
            rate_sems.at[0, d],
            rate_sems.at[1, d],
            {"tm": 2 * later_z(d) + c},
        )
        copy.start()
        rate_copies.append(copy)

    project(0)

    head = HALF * c + (row * SHARE + lax.broadcasted_iota(jnp.int32, (SHARE, DH), 0)) // DH

    def expand(tile):
        factor = jnp.zeros((SHARE, DH), F32)
        for h in range(HEADS):
            factor = jnp.where(head == h, tile[h : h + 1, :], factor)
        return factor

    summed = kv_buf[row].astype(F32)
    for d in range(1, ROW):
        reduces[d - 1].wait()
        summed = summed + parts[d].astype(F32)
    first, second = summed[:SHARE], summed[SHARE:]
    first_rate, second_rate = expand(rates[0]), expand(rates[1])
    pair_kv[...] = (second_rate * first + second).astype(BF)
    scans = []
    for d in range(1, ZS):
        copy = remote(
            pair_kv,
            scan_kv.at[d],
            scan_sems.at[0, d],
            scan_sems.at[1, d],
            {"tm": 2 * later_z(d) + c},
        )
        copy.start()
        scans.append(copy)
    for copy in rate_copies:
        copy.wait()
    for copy in scans:
        copy.wait()

    def advance(zi, running):
        d = z - zi
        return expand(scan_rate[d]) * running + scan_kv[d].astype(F32)

    running = lax.fori_loop(0, z, advance, jnp.zeros((SHARE, DH), F32))
    first_state = first_rate * running + first
    second_state = second_rate * first_state + second
    state_share[...] = jnp.concatenate([first_state, second_state], axis=0).astype(BF)

    gathers = []
    for d in range(1, ROW):
        copy = remote(
            state_share,
            state_buf.at[row],
            state_sems.at[0, d],
            state_sems.at[1, d],
            {"row": lax.rem(row + d, ROW)},
        )
        copy.start()
        gathers.append(copy)
    state_buf[row] = state_share[...]
    for d in range(1, ROW):
        sender = lax.rem(row - d + ROW, ROW)
        remote(
            state_share,
            state_buf.at[sender],
            state_sems.at[0, d],
            state_sems.at[1, d],
            {"row": sender},
        ).wait_recv()

    states = state_buf[...].astype(F32)
    by_frame = [
        states[:, :SHARE].reshape(WIDE, DH).astype(BF),
        states[:, SHARE:].reshape(WIDE, DH).astype(BF),
    ]
    base = pl.multiple_of(c * WIDE, DH)

    def attended(frame, h):
        queries = projected[frame * 256 : (frame + 1) * 256, h * DH : (h + 1) * DH]
        found = jnp.dot(
            queries, by_frame[frame][h * DH : (h + 1) * DH, :], preferred_element_type=F32
        )
        scale = lax.rsqrt(jnp.mean(found * found, axis=-1, keepdims=True) + 1e-06)
        return (found * scale).astype(BF)

    for frame in range(2):
        for h in range(HALF):
            mixed_out[frame, :, h * DH : (h + 1) * DH] = attended(frame, h)
    final = remote(
        mixed_out.at[other], mixed_in, near_sems.at[0, 4], near_sems.at[1, 4], {"tm": sibling}
    )
    final.start()
    out_ref[:, pl.ds(base, WIDE)] = mixed_out[c]

    @pl.when(c == parity)
    def _():
        for copy in scatter(block, main_send, main_recv):
            copy.wait_send()

    @pl.when(c == last_parity)
    def _():
        for copy in scatter(last_block, last_send, last_recv):
            copy.wait_send()

    for copy in gathers:
        copy.wait_send()
    final.wait()
    out_ref[:, pl.ds(pl.multiple_of(other * WIDE, DH), WIDE)] = mixed_in[...]


def run(video, last, weights, stem, decay_tile):
    dma = pltpu.SemaphoreType.DMA
    vmem = pltpu.VMEM
    return pl.pallas_call(
        kernel,
        out_shape=jax.ShapeDtypeStruct((256, HEADS * DH), BF),
        in_specs=[pl.BlockSpec(memory_space=pltpu.VMEM)] * 5,
        out_specs=pl.BlockSpec(memory_space=pltpu.VMEM),
        scratch_shapes=[
            vmem((2, 112, 1024), BF),
            vmem((ZS, 2, DEPTH, COLS), BF),
            vmem((1152, 1536), BF),
            vmem((576, 1536), BF),
            vmem((512, 1536), BF),
            vmem((512, COLS), BF),
            vmem((2, 8, 128), F32),
            vmem((8, 128), F32),
            vmem((ROW, 2 * SHARE, DH), BF),
            vmem((ROW, 2 * SHARE, DH), BF),
            vmem((SHARE, DH), BF),
            vmem((ZS, SHARE, DH), BF),
            vmem((ZS, 8, 128), F32),
            vmem((2 * SHARE, DH), BF),
            vmem((ROW, 2 * SHARE, DH), BF),
            vmem((2, 256, WIDE), BF),
            vmem((256, WIDE), BF),
            dma((2, 5)),
            dma((2, ZS)),
            dma((ZS,)),
            dma((2, ZS)),
            dma((ZS,)),
            dma((2, 4, 2, SIDE)),
            dma((2, 4, 2, SIDE, SIDE)),
            dma((2,)),
            dma((2, ROW)),
            dma((2, ZS)),
            dma((2, ZS)),
            dma((2, ROW)),
        ],
        compiler_params=pltpu.CompilerParams(collective_id=0, has_side_effects=True),
        name="frames",
    )(video, last, weights, stem, decay_tile)


def local(video, stem_weight, w_qkv, decay):
    image = video.reshape(96, 1024)
    last = jnp.pad(video[0, :, -1, :], ((0, 12), (0, 0)))
    stem = jnp.pad(stem_weight.reshape(64, 36).T, ((0, 12), (0, 0)))
    decay_tile = jnp.pad(jnp.broadcast_to(decay.reshape(HEADS, 1), (HEADS, 128)), ((0, 2), (0, 0)))
    mixed = run(image, last, w_qkv, stem, decay_tile)
    return mixed.reshape(1, 2, 128, HEADS * DH)


def solution(mesh):
    return jax.shard_map(
        local,
        mesh=mesh,
        in_specs=(P("tm", None, "row", None), P(), P("tm", None), P("tm", None)),
        out_specs=P("tm", "row", None, None),
        check_vma=False,
    )
```

```python
import jax
import jax.numpy as jnp
from jax import lax
from jax.experimental import pallas as pl
from jax.experimental.pallas import tpu as pltpu
from jax.sharding import PartitionSpec as P

HEADS = 6
HALF = 3
DH = 128
ROW = 16
SIDE = 4
ZS = 16
SHARE = 24
WIDE = HALF * DH
COLS = 3 * WIDE
DEPTH = 48
MESH = pl.DeviceIdType.MESH
BF = jnp.bfloat16
F32 = jnp.float32


def remote(src, dst, send, recv, where):
    return pltpu.make_async_remote_copy(
        src_ref=src,
        dst_ref=dst,
        send_sem=send,
        recv_sem=recv,
        device_id=where,
        device_id_type=MESH,
    )


def one_hot(rows, columns, target, axis):
    places = lax.broadcasted_iota(jnp.int32, (rows, columns), axis)
    return jnp.where(places == target, 1.0, 0.0).astype(BF)


def kernel(
    decay_ref,
    video_ref,
    w_ref,
    stem_ref,
    out_ref,
    images,
    last_rows,
    own_rate,
    wbuf,
    spread,
    stem,
    tokens,
    projected,
    rates,
    pair_rate,
    kv_buf,
    parts,
    pair_kv,
    scan_kv,
    scan_rate,
    state_share,
    state_buf,
    mixed_out,
    mixed_in,
    near_sems,
    main_sems,
    main_next,
    last_sems,
    last_next,
    own_sems,
    pass_sems,
    swap_sems,
    row_sems,
    rate_sems,
    scan_sems,
    state_sems,
):
    tm = lax.axis_index("tm")
    row = lax.axis_index("row")
    z, c = tm // 2, lax.rem(tm, 2)
    x, y = row // SIDE, lax.rem(row, SIDE)
    sibling = tm + 1 - 2 * c
    other = 1 - c
    below = lax.rem(row + 1, ROW)
    above = lax.rem(row + ROW - 1, ROW)
    parity = lax.rem(row, 2)
    block = row // 2
    last_parity = lax.rem(x, 2)

    barrier = pltpu.get_barrier_semaphore()

    def greet(where):
        pl.semaphore_signal(barrier, inc=1, device_id=where, device_id_type=MESH)

    def later_z(d):
        return lax.rem(z + d, ZS)

    def earlier_z(d):
        return lax.rem(z - d + ZS, ZS)

    for d in range(1, ZS):
        greet({"tm": 2 * later_z(d) + c})
    for d in (4, 8, 12):
        greet({"tm": 2 * later_z(d) + other})
    greet({"tm": sibling})
    for d in range(1, ROW):
        greet({"row": lax.rem(row + d, ROW)})
    greet({"tm": sibling, "row": below})
    greet({"tm": sibling, "row": above})

    def source(b, t):
        part = b // HALF
        start = part * HEADS * DH + t * WIDE + (b - part * HALF) * DH
        return w_ref.at[:, pl.ds(pl.multiple_of(start, DH), DH)]

    def place(zi, ci, b):
        return wbuf.at[
            zi // 4, lax.rem(zi, 4), ci, :, pl.ds(pl.multiple_of(b * DH, DH), DH)
        ]

    line = lax.broadcasted_iota(jnp.int32, (16, 1), 0)
    last_pick = one_hot(16, 96, jnp.where(line < 4, 24 * line + 23, -1), 1)
    last_rows[...] = jnp.dot(last_pick, video_ref[...], preferred_element_type=F32).astype(BF)
    place_of = lax.broadcasted_iota(jnp.int32, (8, 128), 0)
    rate = jnp.zeros((8, 128), F32)
    for h in range(HEADS):
        rate = jnp.where(place_of == h, decay_ref[0, h], rate)
    own_rate[...] = rate
    rates[c] = rate

    pl.semaphore_wait(barrier, ZS - 1 + 3 + 1 + ROW - 1 + 2)

    near = [
        remote(video_ref, images.at[c, 0:96], near_sems.at[0, 0], near_sems.at[1, 0], {"tm": sibling}),
        remote(last_rows, images.at[c, 96:112], near_sems.at[0, 1], near_sems.at[1, 1], {"row": below}),
        remote(
            last_rows,
            images.at[c, 96:112],
            near_sems.at[0, 2],
            near_sems.at[1, 2],
            {"tm": sibling, "row": below},
        ),
        remote(own_rate, rates.at[c], near_sems.at[0, 3], near_sems.at[1, 3], {"tm": sibling}),
    ]
    for copy in near:
        copy.start()

    def scatter(b, sems):
        copies = []
        for k in range(1, 4):
            for t in range(2):
                copies.append(
                    remote(
                        source(b, t),
                        place(z, c, b),
                        sems.at[0, t, k],
                        sems.at[1, 0, k],
                        {"tm": 2 * later_z(4 * k) + t},
                    )
                )
        copies.append(
            remote(
                source(b, other), place(z, c, b), sems.at[0, 0, 0], sems.at[1, 0, 0], {"tm": sibling}
            )
        )
        return copies

    def scattered(b, ci, sems):
        for k in range(1, 4):
            spot = place(earlier_z(4 * k), ci, b)
            remote(spot, spot, sems.at[0, 0, k], sems.at[1, 0, k], {"tm": sibling}).wait_recv()

        @pl.when(c != ci)
        def _():
            spot = place(z, ci, b)
            remote(spot, spot, sems.at[0, 0, 0], sems.at[1, 0, 0], {"tm": sibling}).wait_recv()

    def column_of(member, ci, b):
        return wbuf.at[:, member, ci, :, pl.ds(pl.multiple_of(b * DH, DH), DH)]

    member = lax.rem(z, 4)
    hops = (0, 1, 15, 2)

    def hand_on(b, ci, sems):
        copies = []
        for k in range(1, 4):
            own = column_of(member, ci, b)
            copies.append(
                remote(own, own, sems.at[0, k], sems.at[1, k], {"tm": 2 * later_z(hops[k]) + c})
            )
        return copies

    def member_of(k):
        return lax.rem(z - hops[k] + ZS, 4)

    def handed(b, ci, sems, k):
        spot = column_of(member_of(k), ci, b)
        remote(spot, spot, sems.at[0, k], sems.at[1, k], {"tm": sibling}).wait_recv()

    last_block = 8

    @pl.when(c == parity)
    def _():
        for copy in scatter(block, main_sems):
            copy.start()
        place(z, c, block)[...] = source(block, c)[...]

    @pl.when(c == last_parity)
    def _():
        place(z, c, last_block)[...] = source(last_block, c)[...]

    images[c, 0:96, :] = video_ref[...]
    copies_of = lax.broadcasted_iota(jnp.int32, (1, 1536), 1)
    channel = copies_of // 24
    position = copies_of - channel * 24
    repeat = one_hot(64, 1536, channel, 0)
    kernels = jnp.dot(stem_ref[...], repeat, preferred_element_type=F32)
    for ij in range(24):
        spread[ij * 48 : (ij + 1) * 48, :] = jnp.where(position == ij, kernels, 0.0).astype(BF)
    term = lax.broadcasted_iota(jnp.int32, (1, 1152), 1)
    ij = term // 48
    fab = term - ij * 48
    i, j = ij // 4, ij - (ij // 4) * 4
    f = fab // 9
    a = (fab - f * 9) // 3
    b = fab - f * 9 - a * 3
    goal = jnp.where(fab < 36, (2 * j + b) * 64 + f * 16 + 2 * i + a, -1)
    chosen = one_hot(576, 1152, goal, 0)
    for n in range(3):
        stem[:, n * 512 : (n + 1) * 512] = jnp.dot(
            chosen, spread[:, n * 512 : (n + 1) * 512], preferred_element_type=F32
        ).astype(BF)

    def piece(k, chip, start, count):
        return wbuf.at[
            start : start + count,
            member_of(k),
            lax.rem(chip, 2),
            :,
            pl.ds(pl.multiple_of((chip // 2) * DH, DH), DH),
        ]

    def chip_at(dx, dy):
        return lax.rem(x + dx + SIDE, SIDE) * SIDE + lax.rem(y + dy + SIDE, SIDE)

    def step(axis, d):
        return chip_at(d, 0) if axis == 0 else chip_at(0, d)

    sent = []

    def send_own(k):
        if k > 0:
            handed(block, parity, main_next, k)
        for d in range(1, SIDE):
            for axis in range(2):
                copy = remote(
                    piece(k, row, 0, 4),
                    piece(k, row, 0, 4),
                    own_sems.at[0, k, axis, d],
                    own_sems.at[1, k, axis, d],
                    {"row": step(axis, d)},
                )
                copy.start()
                sent.append(copy)

    def pass_on(k):
        for e in range(1, SIDE):
            for axis in range(2):
                origin = step(axis, -e)
                here = piece(k, origin, 0, 4)
                remote(
                    here, here, own_sems.at[0, k, axis, e], own_sems.at[1, k, axis, e], {"row": origin}
                ).wait_recv()
                half = piece(k, origin, 2 * axis, 2)
                for d in range(1, SIDE):
                    copy = remote(
                        half,
                        half,
                        pass_sems.at[0, k, axis, d, e],
                        pass_sems.at[1, k, axis, d, e],
                        {"row": step(1 - axis, d)},
                    )
                    copy.start()
                    sent.append(copy)

    scattered(block, parity, main_sems)
    handing = hand_on(block, parity, main_next)
    for copy in handing:
        copy.start()
    send_own(0)

    @pl.when(c == last_parity)
    def _():
        for copy in scatter(last_block, last_sems):
            copy.start()

    for copy in near:
        copy.wait()

    line = lax.broadcasted_iota(jnp.int32, (128, 1), 0)
    patch, field, tap = line // 64, lax.rem(line, 64) // 16, lax.rem(line, 16)
    image_row = 12 * patch - 1 + tap
    above_row = jnp.where(row == 0, -1, 96 + field)
    picked = jnp.where(image_row < 0, above_row, field * 24 + image_row)
    picked = jnp.where(tap > 12, -1, picked)
    row_pick = one_hot(128, 112, picked, 1)
    column = lax.broadcasted_iota(jnp.int32, (1, 1152), 1)
    tap_column = 8 * lax.rem(column, 128) - 1 + column // 128
    column_pick = one_hot(1024, 1152, tap_column, 0)
    pair_rate[...] = rates[0] * rates[1]
    for frame in range(2):
        rows_of = jnp.dot(row_pick, images[frame], preferred_element_type=F32).astype(BF)
        taps = jnp.dot(rows_of, column_pick, preferred_element_type=F32).astype(BF)
        for p in range(2):
            stacked = jnp.concatenate(
                [taps[p * 64 : (p + 1) * 64, k * 128 : (k + 1) * 128] for k in range(9)], axis=0
            )
            at = (frame * 2 + p) * 128
            for n in range(3):
                made = lax.dot_general(
                    stacked,
                    stem[:, n * 512 : (n + 1) * 512],
                    (((0,), (0,)), ((), ())),
                    preferred_element_type=F32,
                )
                tokens[at : at + 128, n * 512 : (n + 1) * 512] = jnp.tanh(made).astype(BF)

    send_own(1)
    pass_on(0)
    scattered(last_block, last_parity, last_sems)
    last_handing = hand_on(last_block, last_parity, last_next)
    for copy in last_handing:
        copy.start()
    send_own(2)
    pass_on(1)
    send_own(3)
    pass_on(2)
    pass_on(3)
    for k in range(1, 4):
        handed(last_block, last_parity, last_next, k)
    mine = wbuf.at[:, :, last_parity, :, last_block * DH : (last_block + 1) * DH]
    neighbour = (x + 1 - 2 * last_parity) * SIDE + y
    swap = remote(mine, mine, swap_sems.at[0], swap_sems.at[1], {"row": neighbour})
    swap.start()

    for k in range(4):
        for axis in range(2):
            for d in range(1, SIDE):
                for e in range(1, SIDE):
                    origin = chip_at(-e, -d) if axis == 0 else chip_at(-d, -e)
                    half = piece(k, origin, 2 * axis, 2)
                    remote(
                        half,
                        half,
                        pass_sems.at[0, k, axis, d, e],
                        pass_sems.at[1, k, axis, d, e],
                        {"row": origin},
                    ).wait_recv()
    swap.wait_send()
    theirs = wbuf.at[:, :, 1 - last_parity, :, last_block * DH : (last_block + 1) * DH]
    remote(theirs, theirs, swap_sems.at[0], swap_sems.at[1], {"row": neighbour}).wait_recv()
    for copy in sent + handing + last_handing:
        copy.wait_send()

    def project(part):
        weights = wbuf[:, :, :, :, part * WIDE : (part + 1) * WIDE].reshape(1536, WIDE)
        projected[:, part * WIDE : (part + 1) * WIDE] = jnp.dot(
            tokens[...], weights, preferred_element_type=F32
        ).astype(BF)

    project(1)
    project(2)

    sums = []
    for frame in range(2):
        heads = []
        for h in range(HALF):
            keys = projected[frame * 256 : (frame + 1) * 256, WIDE + h * DH : WIDE + (h + 1) * DH]
            values = projected[
                frame * 256 : (frame + 1) * 256, 2 * WIDE + h * DH : 2 * WIDE + (h + 1) * DH
            ]
            heads.append(
                lax.dot_general(
                    keys, values, (((0,), (0,)), ((), ())), preferred_element_type=F32
                )
            )
        sums.append(jnp.concatenate(heads, axis=0).reshape(ROW, SHARE, DH))
    kv_buf[...] = jnp.concatenate(sums, axis=1).astype(BF)

    reduces = []
    for d in range(1, ROW):
        peer = lax.rem(row + d, ROW)
        copy = remote(
            kv_buf.at[peer], parts.at[d], row_sems.at[0, d], row_sems.at[1, d], {"row": peer}
        )
        copy.start()
        reduces.append(copy)
    rate_copies = []
    for d in range(1, ZS):
        copy = remote(
            pair_rate,
            scan_rate.at[d],
            rate_sems.at[0, d],
            rate_sems.at[1, d],
            {"tm": 2 * later_z(d) + c},
        )
        copy.start()
        rate_copies.append(copy)

    project(0)

    head = HALF * c + (row * SHARE + lax.broadcasted_iota(jnp.int32, (SHARE, DH), 0)) // DH

    def expand(tile):
        factor = jnp.zeros((SHARE, DH), F32)
        for h in range(HEADS):
            factor = jnp.where(head == h, tile[h : h + 1, :], factor)
        return factor

    summed = kv_buf[row].astype(F32)
    for d in range(1, ROW):
        reduces[d - 1].wait()
        summed = summed + parts[d].astype(F32)
    first, second = summed[:SHARE], summed[SHARE:]
    first_rate, second_rate = expand(rates[0]), expand(rates[1])
    pair_kv[...] = (second_rate * first + second).astype(BF)
    scans = []
    for d in range(1, ZS):
        copy = remote(
            pair_kv,
            scan_kv.at[d],
            scan_sems.at[0, d],
            scan_sems.at[1, d],
            {"tm": 2 * later_z(d) + c},
        )
        copy.start()
        scans.append(copy)
    for copy in rate_copies:
        copy.wait()
    for copy in scans:
        copy.wait()

    def advance(zi, running):
        d = z - zi
        return expand(scan_rate[d]) * running + scan_kv[d].astype(F32)

    running = lax.fori_loop(0, z, advance, jnp.zeros((SHARE, DH), F32))
    first_state = first_rate * running + first
    second_state = second_rate * first_state + second
    state_share[...] = jnp.concatenate([first_state, second_state], axis=0).astype(BF)

    gathers = []
    for d in range(1, ROW):
        copy = remote(
            state_share,
            state_buf.at[row],
            state_sems.at[0, d],
            state_sems.at[1, d],
            {"row": lax.rem(row + d, ROW)},
        )
        copy.start()
        gathers.append(copy)
    state_buf[row] = state_share[...]
    for d in range(1, ROW):
        sender = lax.rem(row - d + ROW, ROW)
        remote(
            state_share,
            state_buf.at[sender],
            state_sems.at[0, d],
            state_sems.at[1, d],
            {"row": sender},
        ).wait_recv()

    states = state_buf[...].astype(F32)
    by_frame = [
        states[:, :SHARE].reshape(WIDE, DH).astype(BF),
        states[:, SHARE:].reshape(WIDE, DH).astype(BF),
    ]
    base = pl.multiple_of(c * WIDE, DH)

    def attended(frame, h):
        queries = projected[frame * 256 : (frame + 1) * 256, h * DH : (h + 1) * DH]
        found = jnp.dot(
            queries, by_frame[frame][h * DH : (h + 1) * DH, :], preferred_element_type=F32
        )
        scale = lax.rsqrt(jnp.mean(found * found, axis=-1, keepdims=True) + 1e-06)
        return (found * scale).astype(BF)

    for frame in range(2):
        for h in range(HALF):
            mixed_out[frame, :, h * DH : (h + 1) * DH] = attended(frame, h)
    final = remote(
        mixed_out.at[other], mixed_in, near_sems.at[0, 4], near_sems.at[1, 4], {"tm": sibling}
    )
    final.start()
    out_ref[:, pl.ds(base, WIDE)] = mixed_out[c]

    @pl.when(c == parity)
    def _():
        for copy in scatter(block, main_sems):
            copy.wait_send()

    @pl.when(c == last_parity)
    def _():
        for copy in scatter(last_block, last_sems):
            copy.wait_send()

    for copy in gathers:
        copy.wait_send()
    final.wait()
    out_ref[:, pl.ds(pl.multiple_of(other * WIDE, DH), WIDE)] = mixed_in[...]


def run(decay, video, weights, stem):
    dma = pltpu.SemaphoreType.DMA
    vmem = pltpu.VMEM
    return pl.pallas_call(
        kernel,
        out_shape=jax.ShapeDtypeStruct((256, HEADS * DH), BF),
        in_specs=[pl.BlockSpec(memory_space=pltpu.SMEM)]
        + [pl.BlockSpec(memory_space=pltpu.VMEM)] * 3,
        out_specs=pl.BlockSpec(memory_space=pltpu.VMEM),
        scratch_shapes=[
            vmem((2, 112, 1024), BF),
            vmem((16, 1024), BF),
            vmem((8, 128), F32),
            vmem((4, 4, 2, DEPTH, COLS), BF),
            vmem((1152, 1536), BF),
            vmem((576, 1536), BF),
            vmem((512, 1536), BF),
            vmem((512, COLS), BF),
            vmem((2, 8, 128), F32),
            vmem((8, 128), F32),
            vmem((ROW, 2 * SHARE, DH), BF),
            vmem((ROW, 2 * SHARE, DH), BF),
            vmem((SHARE, DH), BF),
            vmem((ZS, SHARE, DH), BF),
            vmem((ZS, 8, 128), F32),
            vmem((2 * SHARE, DH), BF),
            vmem((ROW, 2 * SHARE, DH), BF),
            vmem((2, 256, WIDE), BF),
            vmem((256, WIDE), BF),
            dma((2, 5)),
            dma((2, 2, 4)),
            dma((2, 4)),
            dma((2, 2, 4)),
            dma((2, 4)),
            dma((2, 4, 2, SIDE)),
            dma((2, 4, 2, SIDE, SIDE)),
            dma((2,)),
            dma((2, ROW)),
            dma((2, ZS)),
            dma((2, ZS)),
            dma((2, ROW)),
        ],
        compiler_params=pltpu.CompilerParams(collective_id=0, has_side_effects=True),
        name="frames",
    )(decay, video, weights, stem)


def local(video, stem_weight, w_qkv, decay):
    image = video.reshape(96, 1024)
    stem = jnp.pad(stem_weight.reshape(64, 36).T, ((0, 12), (0, 0)))
    mixed = run(decay, image, w_qkv, stem)
    return mixed.reshape(1, 2, 128, HEADS * DH)


def solution(mesh):
    return jax.shard_map(
        local,
        mesh=mesh,
        in_specs=(P("tm", None, "row", None), P(), P("tm", None), P("tm", None)),
        out_specs=P("tm", "row", None, None),
        check_vma=False,
    )
```

```python
import jax
import jax.numpy as jnp
from jax import lax
from jax.experimental import pallas as pl
from jax.experimental.pallas import tpu as pltpu
from jax.sharding import PartitionSpec as P

HEADS = 6
HALF = 3
DH = 128
ROW = 16
SIDE = 4
ZS = 16
SHARE = 24
WIDE = HALF * DH
COLS = 3 * WIDE
DEPTH = 48
MESH = pl.DeviceIdType.MESH
BF = jnp.bfloat16
F32 = jnp.float32


def remote(src, dst, send, recv, where):
    return pltpu.make_async_remote_copy(
        src_ref=src,
        dst_ref=dst,
        send_sem=send,
        recv_sem=recv,
        device_id=where,
        device_id_type=MESH,
    )


def one_hot(rows, columns, target, axis):
    places = lax.broadcasted_iota(jnp.int32, (rows, columns), axis)
    return jnp.where(places == target, 1.0, 0.0).astype(BF)


def kernel(
    decay_ref,
    video_ref,
    w_ref,
    stem_ref,
    out_ref,
    images,
    last_rows,
    own_rate,
    wbuf,
    spread,
    stem,
    tokens,
    projected,
    rates,
    pair_rate,
    kv_buf,
    parts,
    pair_kv,
    scan_kv,
    scan_rate,
    state_share,
    state_buf,
    mixed_out,
    mixed_in,
    near_sems,
    main_sems,
    main_next,
    last_sems,
    last_next,
    own_sems,
    pass_sems,
    swap_sems,
    row_sems,
    rate_sems,
    scan_sems,
    state_sems,
):
    tm = lax.axis_index("tm")
    row = lax.axis_index("row")
    z, c = tm // 2, lax.rem(tm, 2)
    x, y = row // SIDE, lax.rem(row, SIDE)
    sibling = tm + 1 - 2 * c
    other = 1 - c
    below = lax.rem(row + 1, ROW)
    above = lax.rem(row + ROW - 1, ROW)
    parity = lax.rem(row, 2)
    block = row // 2
    last_parity = lax.rem(x, 2)

    barrier = pltpu.get_barrier_semaphore()

    def greet(where):
        pl.semaphore_signal(barrier, inc=1, device_id=where, device_id_type=MESH)

    def later_z(d):
        return lax.rem(z + d, ZS)

    def earlier_z(d):
        return lax.rem(z - d + ZS, ZS)

    for d in range(1, ZS):
        greet({"tm": 2 * later_z(d) + c})
    for d in (4, 8, 12):
        greet({"tm": 2 * later_z(d) + other})
    greet({"tm": sibling})
    for d in range(1, ROW):
        greet({"row": lax.rem(row + d, ROW)})
    greet({"tm": sibling, "row": below})
    greet({"tm": sibling, "row": above})

    def source(b, t):
        part = b // HALF
        start = part * HEADS * DH + t * WIDE + (b - part * HALF) * DH
        return w_ref.at[:, pl.ds(pl.multiple_of(start, DH), DH)]

    def place(zi, ci, b):
        return wbuf.at[
            zi // 4, lax.rem(zi, 4), ci, :, pl.ds(pl.multiple_of(b * DH, DH), DH)
        ]

    line = lax.broadcasted_iota(jnp.int32, (16, 1), 0)
    last_pick = one_hot(16, 96, jnp.where(line < 4, 24 * line + 23, -1), 1)
    last_rows[...] = jnp.dot(last_pick, video_ref[...], preferred_element_type=F32).astype(BF)
    place_of = lax.broadcasted_iota(jnp.int32, (8, 128), 0)
    rate = jnp.zeros((8, 128), F32)
    for h in range(HEADS):
        rate = jnp.where(place_of == h, decay_ref[0, h], rate)
    own_rate[...] = rate
    rates[c] = rate

    pl.semaphore_wait(barrier, ZS - 1 + 3 + 1 + ROW - 1 + 2)

    near = [
        remote(video_ref, images.at[c, 0:96], near_sems.at[0, 0], near_sems.at[1, 0], {"tm": sibling}),
        remote(last_rows, images.at[c, 96:112], near_sems.at[0, 1], near_sems.at[1, 1], {"row": below}),
        remote(
            last_rows,
            images.at[c, 96:112],
            near_sems.at[0, 2],
            near_sems.at[1, 2],
            {"tm": sibling, "row": below},
        ),
        remote(own_rate, rates.at[c], near_sems.at[0, 3], near_sems.at[1, 3], {"tm": sibling}),
    ]
    for copy in near:
        copy.start()

    def scatter(b, sems):
        copies = []
        for k in range(1, 4):
            for t in range(2):
                copies.append(
                    remote(
                        source(b, t),
                        place(z, c, b),
                        sems.at[0, t, k],
                        sems.at[1, 0, k],
                        {"tm": 2 * later_z(4 * k) + t},
                    )
                )
        copies.append(
            remote(
                source(b, other), place(z, c, b), sems.at[0, 0, 0], sems.at[1, 0, 0], {"tm": sibling}
            )
        )
        return copies

    def scattered(b, ci, sems):
        for k in range(1, 4):
            spot = place(earlier_z(4 * k), ci, b)
            remote(spot, spot, sems.at[0, 0, k], sems.at[1, 0, k], {"tm": sibling}).wait_recv()

        @pl.when(c != ci)
        def _():
            spot = place(z, ci, b)
            remote(spot, spot, sems.at[0, 0, 0], sems.at[1, 0, 0], {"tm": sibling}).wait_recv()

    def column_of(member, ci, b):
        return wbuf.at[:, member, ci, :, pl.ds(pl.multiple_of(b * DH, DH), DH)]

    member = lax.rem(z, 4)
    hops = (0, 1, 15, 2)

    def hand_on(b, ci, sems):
        copies = []
        for k in range(1, 4):
            own = column_of(member, ci, b)
            copies.append(
                remote(own, own, sems.at[0, k], sems.at[1, k], {"tm": 2 * later_z(hops[k]) + c})
            )
        return copies

    def member_of(k):
        return lax.rem(z - hops[k] + ZS, 4)

    def handed(b, ci, sems, k):
        spot = column_of(member_of(k), ci, b)
        remote(spot, spot, sems.at[0, k], sems.at[1, k], {"tm": sibling}).wait_recv()

    last_block = 8

    @pl.when(c == parity)
    def _():
        for copy in scatter(block, main_sems):
            copy.start()
        place(z, c, block)[...] = source(block, c)[...]

    @pl.when(c == last_parity)
    def _():
        place(z, c, last_block)[...] = source(last_block, c)[...]

    images[c, 0:96, :] = video_ref[...]
    copies_of = lax.broadcasted_iota(jnp.int32, (1, 1536), 1)
    channel = copies_of // 24
    position = copies_of - channel * 24
    repeat = one_hot(64, 1536, channel, 0)
    kernels = jnp.dot(stem_ref[...], repeat, preferred_element_type=F32)
    for ij in range(24):
        spread[ij * 48 : (ij + 1) * 48, :] = jnp.where(position == ij, kernels, 0.0).astype(BF)
    def piece(k, chip, start, count):
        return wbuf.at[
            start : start + count,
            member_of(k),
            lax.rem(chip, 2),
            :,
            pl.ds(pl.multiple_of((chip // 2) * DH, DH), DH),
        ]

    def chip_at(dx, dy):
        return lax.rem(x + dx + SIDE, SIDE) * SIDE + lax.rem(y + dy + SIDE, SIDE)

    def step(axis, d):
        return chip_at(d, 0) if axis == 0 else chip_at(0, d)

    sent = []

    def send_own(k):
        if k > 0:
            handed(block, parity, main_next, k)
        for d in range(1, SIDE):
            for axis in range(2):
                copy = remote(
                    piece(k, row, 0, 4),
                    piece(k, row, 0, 4),
                    own_sems.at[0, k, axis, d],
                    own_sems.at[1, k, axis, d],
                    {"row": step(axis, d)},
                )
                copy.start()
                sent.append(copy)

    def pass_on(k):
        for e in range(1, SIDE):
            for axis in range(2):
                origin = step(axis, -e)
                here = piece(k, origin, 0, 4)
                remote(
                    here, here, own_sems.at[0, k, axis, e], own_sems.at[1, k, axis, e], {"row": origin}
                ).wait_recv()
                half = piece(k, origin, 2 * axis, 2)
                for d in range(1, SIDE):
                    copy = remote(
                        half,
                        half,
                        pass_sems.at[0, k, axis, d, e],
                        pass_sems.at[1, k, axis, d, e],
                        {"row": step(1 - axis, d)},
                    )
                    copy.start()
                    sent.append(copy)

    scattered(block, parity, main_sems)
    handing = hand_on(block, parity, main_next)
    for copy in handing:
        copy.start()
    send_own(0)

    @pl.when(c == last_parity)
    def _():
        for copy in scatter(last_block, last_sems):
            copy.start()

    term = lax.broadcasted_iota(jnp.int32, (1, 1152), 1)
    ij = term // 48
    fab = term - ij * 48
    i, j = ij // 4, ij - (ij // 4) * 4
    f = fab // 9
    a = (fab - f * 9) // 3
    b = fab - f * 9 - a * 3
    goal = jnp.where(fab < 36, (2 * j + b) * 64 + f * 16 + 2 * i + a, -1)
    chosen = one_hot(576, 1152, goal, 0)
    for n in range(3):
        stem[:, n * 512 : (n + 1) * 512] = jnp.dot(
            chosen, spread[:, n * 512 : (n + 1) * 512], preferred_element_type=F32
        ).astype(BF)

    send_own(1)
    pass_on(0)

    for copy in near:
        copy.wait()

    line = lax.broadcasted_iota(jnp.int32, (128, 1), 0)
    patch, field, tap = line // 64, lax.rem(line, 64) // 16, lax.rem(line, 16)
    image_row = 12 * patch - 1 + tap
    above_row = jnp.where(row == 0, -1, 96 + field)
    picked = jnp.where(image_row < 0, above_row, field * 24 + image_row)
    picked = jnp.where(tap > 12, -1, picked)
    row_pick = one_hot(128, 112, picked, 1)
    column = lax.broadcasted_iota(jnp.int32, (1, 1152), 1)
    tap_column = 8 * lax.rem(column, 128) - 1 + column // 128
    column_pick = one_hot(1024, 1152, tap_column, 0)
    pair_rate[...] = rates[0] * rates[1]
    def embed(frame):
        rows_of = jnp.dot(row_pick, images[frame], preferred_element_type=F32).astype(BF)
        taps = jnp.dot(rows_of, column_pick, preferred_element_type=F32).astype(BF)
        for p in range(2):
            stacked = jnp.concatenate(
                [taps[p * 64 : (p + 1) * 64, k * 128 : (k + 1) * 128] for k in range(9)], axis=0
            )
            at = (frame * 2 + p) * 128
            for n in range(3):
                made = lax.dot_general(
                    stacked,
                    stem[:, n * 512 : (n + 1) * 512],
                    (((0,), (0,)), ((), ())),
                    preferred_element_type=F32,
                )
                tokens[at : at + 128, n * 512 : (n + 1) * 512] = jnp.tanh(made).astype(BF)

    neighbour = (x + 1 - 2 * last_parity) * SIDE + y

    def swap(k, ci):
        spot = wbuf.at[:, member_of(k), ci, :, last_block * DH : (last_block + 1) * DH]
        return remote(spot, spot, swap_sems.at[0, k], swap_sems.at[1, k], {"row": neighbour})

    embed(0)
    send_own(2)
    pass_on(1)
    scattered(last_block, last_parity, last_sems)
    last_handing = hand_on(last_block, last_parity, last_next)
    for copy in last_handing:
        copy.start()
    swap(0, last_parity).start()
    embed(1)
    send_own(3)
    pass_on(2)
    for k in range(1, 4):
        handed(last_block, last_parity, last_next, k)
        swap(k, last_parity).start()
    pass_on(3)

    for k in range(4):
        for axis in range(2):
            for d in range(1, SIDE):
                for e in range(1, SIDE):
                    origin = chip_at(-e, -d) if axis == 0 else chip_at(-d, -e)
                    half = piece(k, origin, 2 * axis, 2)
                    remote(
                        half,
                        half,
                        pass_sems.at[0, k, axis, d, e],
                        pass_sems.at[1, k, axis, d, e],
                        {"row": origin},
                    ).wait_recv()
    for k in range(4):
        swap(k, 1 - last_parity).wait_recv()
        swap(k, last_parity).wait_send()
    for copy in sent + handing + last_handing:
        copy.wait_send()

    def project(part):
        weights = wbuf[:, :, :, :, part * WIDE : (part + 1) * WIDE].reshape(1536, WIDE)
        projected[:, part * WIDE : (part + 1) * WIDE] = jnp.dot(
            tokens[...], weights, preferred_element_type=F32
        ).astype(BF)

    project(1)
    project(2)

    sums = []
    for frame in range(2):
        heads = []
        for h in range(HALF):
            keys = projected[frame * 256 : (frame + 1) * 256, WIDE + h * DH : WIDE + (h + 1) * DH]
            values = projected[
                frame * 256 : (frame + 1) * 256, 2 * WIDE + h * DH : 2 * WIDE + (h + 1) * DH
            ]
            heads.append(
                lax.dot_general(
                    keys, values, (((0,), (0,)), ((), ())), preferred_element_type=F32
                )
            )
        sums.append(jnp.concatenate(heads, axis=0).reshape(ROW, SHARE, DH))
    kv_buf[...] = jnp.concatenate(sums, axis=1).astype(BF)

    reduces = []
    for d in range(1, ROW):
        peer = lax.rem(row + d, ROW)
        copy = remote(
            kv_buf.at[peer], parts.at[d], row_sems.at[0, d], row_sems.at[1, d], {"row": peer}
        )
        copy.start()
        reduces.append(copy)
    rate_copies = []
    for d in range(1, ZS):
        copy = remote(
            pair_rate,
            scan_rate.at[d],
            rate_sems.at[0, d],
            rate_sems.at[1, d],
            {"tm": 2 * later_z(d) + c},
        )
        copy.start()
        rate_copies.append(copy)

    project(0)

    head = HALF * c + (row * SHARE + lax.broadcasted_iota(jnp.int32, (SHARE, DH), 0)) // DH

    def expand(tile):
        factor = jnp.zeros((SHARE, DH), F32)
        for h in range(HEADS):
            factor = jnp.where(head == h, tile[h : h + 1, :], factor)
        return factor

    summed = kv_buf[row].astype(F32)
    for d in range(1, ROW):
        reduces[d - 1].wait()
        summed = summed + parts[d].astype(F32)
    first, second = summed[:SHARE], summed[SHARE:]
    first_rate, second_rate = expand(rates[0]), expand(rates[1])
    pair_kv[...] = (second_rate * first + second).astype(BF)
    scans = []
    for d in range(1, ZS):
        copy = remote(
            pair_kv,
            scan_kv.at[d],
            scan_sems.at[0, d],
            scan_sems.at[1, d],
            {"tm": 2 * later_z(d) + c},
        )
        copy.start()
        scans.append(copy)
    for copy in rate_copies:
        copy.wait()
    for copy in scans:
        copy.wait()

    def advance(zi, running):
        d = z - zi
        return expand(scan_rate[d]) * running + scan_kv[d].astype(F32)

    running = lax.fori_loop(0, z, advance, jnp.zeros((SHARE, DH), F32))
    first_state = first_rate * running + first
    second_state = second_rate * first_state + second
    state_share[...] = jnp.concatenate([first_state, second_state], axis=0).astype(BF)

    gathers = []
    for d in range(1, ROW):
        copy = remote(
            state_share,
            state_buf.at[row],
            state_sems.at[0, d],
            state_sems.at[1, d],
            {"row": lax.rem(row + d, ROW)},
        )
        copy.start()
        gathers.append(copy)
    state_buf[row] = state_share[...]
    for d in range(1, ROW):
        sender = lax.rem(row - d + ROW, ROW)
        remote(
            state_share,
            state_buf.at[sender],
            state_sems.at[0, d],
            state_sems.at[1, d],
            {"row": sender},
        ).wait_recv()

    states = state_buf[...].astype(F32)
    by_frame = [
        states[:, :SHARE].reshape(WIDE, DH).astype(BF),
        states[:, SHARE:].reshape(WIDE, DH).astype(BF),
    ]
    base = pl.multiple_of(c * WIDE, DH)

    def attended(frame, h):
        queries = projected[frame * 256 : (frame + 1) * 256, h * DH : (h + 1) * DH]
        found = jnp.dot(
            queries, by_frame[frame][h * DH : (h + 1) * DH, :], preferred_element_type=F32
        )
        scale = lax.rsqrt(jnp.mean(found * found, axis=-1, keepdims=True) + 1e-06)
        return (found * scale).astype(BF)

    for frame in range(2):
        for h in range(HALF):
            mixed_out[frame, :, h * DH : (h + 1) * DH] = attended(frame, h)
    final = remote(
        mixed_out.at[other], mixed_in, near_sems.at[0, 4], near_sems.at[1, 4], {"tm": sibling}
    )
    final.start()
    out_ref[:, pl.ds(base, WIDE)] = mixed_out[c]

    @pl.when(c == parity)
    def _():
        for copy in scatter(block, main_sems):
            copy.wait_send()

    @pl.when(c == last_parity)
    def _():
        for copy in scatter(last_block, last_sems):
            copy.wait_send()

    for copy in gathers:
        copy.wait_send()
    final.wait()
    out_ref[:, pl.ds(pl.multiple_of(other * WIDE, DH), WIDE)] = mixed_in[...]


def run(decay, video, weights, stem):
    dma = pltpu.SemaphoreType.DMA
    vmem = pltpu.VMEM
    return pl.pallas_call(
        kernel,
        out_shape=jax.ShapeDtypeStruct((256, HEADS * DH), BF),
        in_specs=[pl.BlockSpec(memory_space=pltpu.SMEM)]
        + [pl.BlockSpec(memory_space=pltpu.VMEM)] * 3,
        out_specs=pl.BlockSpec(memory_space=pltpu.VMEM),
        scratch_shapes=[
            vmem((2, 112, 1024), BF),
            vmem((16, 1024), BF),
            vmem((8, 128), F32),
            vmem((4, 4, 2, DEPTH, COLS), BF),
            vmem((1152, 1536), BF),
            vmem((576, 1536), BF),
            vmem((512, 1536), BF),
            vmem((512, COLS), BF),
            vmem((2, 8, 128), F32),
            vmem((8, 128), F32),
            vmem((ROW, 2 * SHARE, DH), BF),
            vmem((ROW, 2 * SHARE, DH), BF),
            vmem((SHARE, DH), BF),
            vmem((ZS, SHARE, DH), BF),
            vmem((ZS, 8, 128), F32),
            vmem((2 * SHARE, DH), BF),
            vmem((ROW, 2 * SHARE, DH), BF),
            vmem((2, 256, WIDE), BF),
            vmem((256, WIDE), BF),
            dma((2, 5)),
            dma((2, 2, 4)),
            dma((2, 4)),
            dma((2, 2, 4)),
            dma((2, 4)),
            dma((2, 4, 2, SIDE)),
            dma((2, 4, 2, SIDE, SIDE)),
            dma((2, 4)),
            dma((2, ROW)),
            dma((2, ZS)),
            dma((2, ZS)),
            dma((2, ROW)),
        ],
        compiler_params=pltpu.CompilerParams(collective_id=0, has_side_effects=True),
        name="frames",
    )(decay, video, weights, stem)


def local(video, stem_weight, w_qkv, decay):
    image = video.reshape(96, 1024)
    stem = jnp.pad(stem_weight.reshape(64, 36).T, ((0, 12), (0, 0)))
    mixed = run(decay, image, w_qkv, stem)
    return mixed.reshape(1, 2, 128, HEADS * DH)


def solution(mesh):
    return jax.shard_map(
        local,
        mesh=mesh,
        in_specs=(P("tm", None, "row", None), P(), P("tm", None), P("tm", None)),
        out_specs=P("tm", "row", None, None),
        check_vma=False,
    )
```

```python
import jax
import jax.numpy as jnp
from jax import lax
from jax.experimental import pallas as pl
from jax.experimental.pallas import tpu as pltpu
from jax.sharding import PartitionSpec as P

HEADS = 6
HALF = 3
DH = 128
ROW = 16
SIDE = 4
ZS = 16
SHARE = 24
WIDE = HALF * DH
COLS = 3 * WIDE
DEPTH = 48
MESH = pl.DeviceIdType.MESH
BF = jnp.bfloat16
F32 = jnp.float32


def remote(src, dst, send, recv, where):
    return pltpu.make_async_remote_copy(
        src_ref=src,
        dst_ref=dst,
        send_sem=send,
        recv_sem=recv,
        device_id=where,
        device_id_type=MESH,
    )


def one_hot(rows, columns, target, axis):
    places = lax.broadcasted_iota(jnp.int32, (rows, columns), axis)
    return jnp.where(places == target, 1.0, 0.0).astype(BF)


def kernel(
    decay_ref,
    video_ref,
    w_ref,
    stem_ref,
    out_ref,
    images,
    last_rows,
    own_rate,
    wbuf,
    spread,
    stem,
    tokens,
    projected,
    rates,
    pair_rate,
    kv_buf,
    parts,
    pair_kv,
    scan_kv,
    scan_rate,
    state_share,
    state_buf,
    mixed_out,
    mixed_in,
    near_sems,
    main_sems,
    main_next,
    last_sems,
    last_next,
    own_sems,
    pass_sems,
    swap_sems,
    row_sems,
    rate_sems,
    scan_sems,
    state_sems,
):
    tm = lax.axis_index("tm")
    row = lax.axis_index("row")
    z, c = tm // 2, lax.rem(tm, 2)
    x, y = row // SIDE, lax.rem(row, SIDE)
    sibling = tm + 1 - 2 * c
    other = 1 - c
    below = lax.rem(row + 1, ROW)
    above = lax.rem(row + ROW - 1, ROW)
    parity = lax.rem(row, 2)
    block = row // 2
    last_parity = lax.rem(x, 2)

    barrier = pltpu.get_barrier_semaphore()

    def greet(where):
        pl.semaphore_signal(barrier, inc=1, device_id=where, device_id_type=MESH)

    def later_z(d):
        return lax.rem(z + d, ZS)

    def earlier_z(d):
        return lax.rem(z - d + ZS, ZS)

    for d in range(1, ZS):
        greet({"tm": 2 * later_z(d) + c})
    for d in (4, 8, 12):
        greet({"tm": 2 * later_z(d) + other})
    greet({"tm": sibling})
    for d in range(1, ROW):
        greet({"row": lax.rem(row + d, ROW)})
    greet({"tm": sibling, "row": below})
    greet({"tm": sibling, "row": above})

    def source(b, t):
        part = b // HALF
        start = part * HEADS * DH + t * WIDE + (b - part * HALF) * DH
        return w_ref.at[:, pl.ds(pl.multiple_of(start, DH), DH)]

    def place(zi, ci, b):
        return wbuf.at[
            zi // 4, lax.rem(zi, 4), ci, :, pl.ds(pl.multiple_of(b * DH, DH), DH)
        ]

    line = lax.broadcasted_iota(jnp.int32, (16, 1), 0)
    last_pick = one_hot(16, 96, jnp.where(line < 4, 24 * line + 23, -1), 1)
    last_rows[...] = jnp.dot(last_pick, video_ref[...], preferred_element_type=F32).astype(BF)
    place_of = lax.broadcasted_iota(jnp.int32, (8, 128), 0)
    rate = jnp.zeros((8, 128), F32)
    for h in range(HEADS):
        rate = jnp.where(place_of == h, decay_ref[0, h], rate)
    own_rate[...] = rate
    rates[c] = rate

    pl.semaphore_wait(barrier, ZS - 1 + 3 + 1 + ROW - 1 + 2)

    near = [
        remote(video_ref, images.at[c, 0:96], near_sems.at[0, 0], near_sems.at[1, 0], {"tm": sibling}),
        remote(last_rows, images.at[c, 96:112], near_sems.at[0, 1], near_sems.at[1, 1], {"row": below}),
        remote(
            last_rows,
            images.at[c, 96:112],
            near_sems.at[0, 2],
            near_sems.at[1, 2],
            {"tm": sibling, "row": below},
        ),
        remote(own_rate, rates.at[c], near_sems.at[0, 3], near_sems.at[1, 3], {"tm": sibling}),
    ]
    for copy in near:
        copy.start()

    def scatter(b, sems):
        copies = []
        for k in range(1, 4):
            for t in range(2):
                copies.append(
                    remote(
                        source(b, t),
                        place(z, c, b),
                        sems.at[0, t, k],
                        sems.at[1, 0, k],
                        {"tm": 2 * later_z(4 * k) + t},
                    )
                )
        copies.append(
            remote(
                source(b, other), place(z, c, b), sems.at[0, 0, 0], sems.at[1, 0, 0], {"tm": sibling}
            )
        )
        return copies

    def scattered(b, ci, sems):
        for k in range(1, 4):
            spot = place(earlier_z(4 * k), ci, b)
            remote(spot, spot, sems.at[0, 0, k], sems.at[1, 0, k], {"tm": sibling}).wait_recv()

        @pl.when(c != ci)
        def _():
            spot = place(z, ci, b)
            remote(spot, spot, sems.at[0, 0, 0], sems.at[1, 0, 0], {"tm": sibling}).wait_recv()

    def column_of(member, ci, b):
        return wbuf.at[:, member, ci, :, pl.ds(pl.multiple_of(b * DH, DH), DH)]

    member = lax.rem(z, 4)
    hops = (0, 1, 15, 2)

    def hand_on(b, ci, sems):
        copies = []
        for k in range(1, 4):
            own = column_of(member, ci, b)
            copies.append(
                remote(own, own, sems.at[0, k], sems.at[1, k], {"tm": 2 * later_z(hops[k]) + c})
            )
        return copies

    def member_of(k):
        return lax.rem(z - hops[k] + ZS, 4)

    def handed(b, ci, sems, k):
        spot = column_of(member_of(k), ci, b)
        remote(spot, spot, sems.at[0, k], sems.at[1, k], {"tm": sibling}).wait_recv()

    last_block = 8

    @pl.when(c == parity)
    def _():
        for copy in scatter(block, main_sems):
            copy.start()
        place(z, c, block)[...] = source(block, c)[...]

    @pl.when(c == last_parity)
    def _():
        place(z, c, last_block)[...] = source(last_block, c)[...]

    images[c, 0:96, :] = video_ref[...]
    copies_of = lax.broadcasted_iota(jnp.int32, (1, 1536), 1)
    channel = copies_of // 24
    position = copies_of - channel * 24
    repeat = one_hot(64, 1536, channel, 0)
    stem_line = lax.broadcasted_iota(jnp.int32, (DEPTH, 1), 0)
    stem_pick = one_hot(DEPTH, 36, stem_line, 1)
    padded = lax.dot_general(
        stem_pick, stem_ref[...], (((1,), (1,)), ((), ())), preferred_element_type=F32
    ).astype(BF)
    kernels = jnp.dot(padded, repeat, preferred_element_type=F32)
    for ij in range(24):
        spread[ij * 48 : (ij + 1) * 48, :] = jnp.where(position == ij, kernels, 0.0).astype(BF)
    term = lax.broadcasted_iota(jnp.int32, (1, 1152), 1)
    ij = term // 48
    fab = term - ij * 48
    i, j = ij // 4, ij - (ij // 4) * 4
    f = fab // 9
    a = (fab - f * 9) // 3
    b = fab - f * 9 - a * 3
    goal = jnp.where(fab < 36, (2 * j + b) * 64 + f * 16 + 2 * i + a, -1)
    chosen = one_hot(576, 1152, goal, 0)
    for n in range(3):
        stem[:, n * 512 : (n + 1) * 512] = jnp.dot(
            chosen, spread[:, n * 512 : (n + 1) * 512], preferred_element_type=F32
        ).astype(BF)

    def piece(k, chip, start, count):
        return wbuf.at[
            start : start + count,
            member_of(k),
            lax.rem(chip, 2),
            :,
            pl.ds(pl.multiple_of((chip // 2) * DH, DH), DH),
        ]

    def chip_at(dx, dy):
        return lax.rem(x + dx + SIDE, SIDE) * SIDE + lax.rem(y + dy + SIDE, SIDE)

    def step(axis, d):
        return chip_at(d, 0) if axis == 0 else chip_at(0, d)

    sent = []

    def send_own(k):
        if k > 0:
            handed(block, parity, main_next, k)
        for d in range(1, SIDE):
            for axis in range(2):
                copy = remote(
                    piece(k, row, 0, 4),
                    piece(k, row, 0, 4),
                    own_sems.at[0, k, axis, d],
                    own_sems.at[1, k, axis, d],
                    {"row": step(axis, d)},
                )
                copy.start()
                sent.append(copy)

    def pass_on(k):
        for e in range(1, SIDE):
            for axis in range(2):
                origin = step(axis, -e)
                here = piece(k, origin, 0, 4)
                remote(
                    here, here, own_sems.at[0, k, axis, e], own_sems.at[1, k, axis, e], {"row": origin}
                ).wait_recv()
                half = piece(k, origin, 2 * axis, 2)
                for d in range(1, SIDE):
                    copy = remote(
                        half,
                        half,
                        pass_sems.at[0, k, axis, d, e],
                        pass_sems.at[1, k, axis, d, e],
                        {"row": step(1 - axis, d)},
                    )
                    copy.start()
                    sent.append(copy)

    scattered(block, parity, main_sems)
    handing = hand_on(block, parity, main_next)
    for copy in handing:
        copy.start()
    send_own(0)

    @pl.when(c == last_parity)
    def _():
        for copy in scatter(last_block, last_sems):
            copy.start()

    for copy in near:
        copy.wait()

    line = lax.broadcasted_iota(jnp.int32, (128, 1), 0)
    patch, field, tap = line // 64, lax.rem(line, 64) // 16, lax.rem(line, 16)
    image_row = 12 * patch - 1 + tap
    above_row = jnp.where(row == 0, -1, 96 + field)
    picked = jnp.where(image_row < 0, above_row, field * 24 + image_row)
    picked = jnp.where(tap > 12, -1, picked)
    row_pick = one_hot(128, 112, picked, 1)
    column = lax.broadcasted_iota(jnp.int32, (1, 1152), 1)
    tap_column = 8 * lax.rem(column, 128) - 1 + column // 128
    column_pick = one_hot(1024, 1152, tap_column, 0)
    pair_rate[...] = rates[0] * rates[1]
    for frame in range(2):
        rows_of = jnp.dot(row_pick, images[frame], preferred_element_type=F32).astype(BF)
        taps = jnp.dot(rows_of, column_pick, preferred_element_type=F32).astype(BF)
        for p in range(2):
            stacked = jnp.concatenate(
                [taps[p * 64 : (p + 1) * 64, k * 128 : (k + 1) * 128] for k in range(9)], axis=0
            )
            at = (frame * 2 + p) * 128
            for n in range(3):
                made = lax.dot_general(
                    stacked,
                    stem[:, n * 512 : (n + 1) * 512],
                    (((0,), (0,)), ((), ())),
                    preferred_element_type=F32,
                )
                tokens[at : at + 128, n * 512 : (n + 1) * 512] = jnp.tanh(made).astype(BF)

    send_own(1)
    pass_on(0)
    scattered(last_block, last_parity, last_sems)
    last_handing = hand_on(last_block, last_parity, last_next)
    for copy in last_handing:
        copy.start()
    send_own(2)
    pass_on(1)
    send_own(3)
    pass_on(2)
    pass_on(3)
    for k in range(1, 4):
        handed(last_block, last_parity, last_next, k)
    mine = wbuf.at[:, :, last_parity, :, last_block * DH : (last_block + 1) * DH]
    neighbour = (x + 1 - 2 * last_parity) * SIDE + y
    swap = remote(mine, mine, swap_sems.at[0], swap_sems.at[1], {"row": neighbour})
    swap.start()

    for k in range(4):
        for axis in range(2):
            for d in range(1, SIDE):
                for e in range(1, SIDE):
                    origin = chip_at(-e, -d) if axis == 0 else chip_at(-d, -e)
                    half = piece(k, origin, 2 * axis, 2)
                    remote(
                        half,
                        half,
                        pass_sems.at[0, k, axis, d, e],
                        pass_sems.at[1, k, axis, d, e],
                        {"row": origin},
                    ).wait_recv()
    swap.wait_send()
    theirs = wbuf.at[:, :, 1 - last_parity, :, last_block * DH : (last_block + 1) * DH]
    remote(theirs, theirs, swap_sems.at[0], swap_sems.at[1], {"row": neighbour}).wait_recv()
    for copy in sent + handing + last_handing:
        copy.wait_send()

    def project(part):
        weights = wbuf[:, :, :, :, part * WIDE : (part + 1) * WIDE].reshape(1536, WIDE)
        projected[:, part * WIDE : (part + 1) * WIDE] = jnp.dot(
            tokens[...], weights, preferred_element_type=F32
        ).astype(BF)

    project(1)
    project(2)

    sums = []
    for frame in range(2):
        heads = []
        for h in range(HALF):
            keys = projected[frame * 256 : (frame + 1) * 256, WIDE + h * DH : WIDE + (h + 1) * DH]
            values = projected[
                frame * 256 : (frame + 1) * 256, 2 * WIDE + h * DH : 2 * WIDE + (h + 1) * DH
            ]
            heads.append(
                lax.dot_general(
                    keys, values, (((0,), (0,)), ((), ())), preferred_element_type=F32
                )
            )
        sums.append(jnp.concatenate(heads, axis=0).reshape(ROW, SHARE, DH))
    kv_buf[...] = jnp.concatenate(sums, axis=1).astype(BF)

    reduces = []
    for d in range(1, ROW):
        peer = lax.rem(row + d, ROW)
        copy = remote(
            kv_buf.at[peer], parts.at[d], row_sems.at[0, d], row_sems.at[1, d], {"row": peer}
        )
        copy.start()
        reduces.append(copy)
    rate_copies = []
    for d in range(1, ZS):
        copy = remote(
            pair_rate,
            scan_rate.at[d],
            rate_sems.at[0, d],
            rate_sems.at[1, d],
            {"tm": 2 * later_z(d) + c},
        )
        copy.start()
        rate_copies.append(copy)

    project(0)

    head = HALF * c + (row * SHARE + lax.broadcasted_iota(jnp.int32, (SHARE, DH), 0)) // DH

    def expand(tile):
        factor = jnp.zeros((SHARE, DH), F32)
        for h in range(HEADS):
            factor = jnp.where(head == h, tile[h : h + 1, :], factor)
        return factor

    summed = kv_buf[row].astype(F32)
    for d in range(1, ROW):
        reduces[d - 1].wait()
        summed = summed + parts[d].astype(F32)
    first, second = summed[:SHARE], summed[SHARE:]
    first_rate, second_rate = expand(rates[0]), expand(rates[1])
    pair_kv[...] = (second_rate * first + second).astype(BF)
    scans = []
    for d in range(1, ZS):
        copy = remote(
            pair_kv,
            scan_kv.at[d],
            scan_sems.at[0, d],
            scan_sems.at[1, d],
            {"tm": 2 * later_z(d) + c},
        )
        copy.start()
        scans.append(copy)
    for copy in rate_copies:
        copy.wait()
    for copy in scans:
        copy.wait()

    def advance(zi, running):
        d = z - zi
        return expand(scan_rate[d]) * running + scan_kv[d].astype(F32)

    running = lax.fori_loop(0, z, advance, jnp.zeros((SHARE, DH), F32))
    first_state = first_rate * running + first
    second_state = second_rate * first_state + second
    state_share[...] = jnp.concatenate([first_state, second_state], axis=0).astype(BF)

    gathers = []
    for d in range(1, ROW):
        copy = remote(
            state_share,
            state_buf.at[row],
            state_sems.at[0, d],
            state_sems.at[1, d],
            {"row": lax.rem(row + d, ROW)},
        )
        copy.start()
        gathers.append(copy)
    state_buf[row] = state_share[...]
    for d in range(1, ROW):
        sender = lax.rem(row - d + ROW, ROW)
        remote(
            state_share,
            state_buf.at[sender],
            state_sems.at[0, d],
            state_sems.at[1, d],
            {"row": sender},
        ).wait_recv()

    states = state_buf[...].astype(F32)
    by_frame = [
        states[:, :SHARE].reshape(WIDE, DH).astype(BF),
        states[:, SHARE:].reshape(WIDE, DH).astype(BF),
    ]
    base = pl.multiple_of(c * WIDE, DH)

    def attended(frame, h):
        queries = projected[frame * 256 : (frame + 1) * 256, h * DH : (h + 1) * DH]
        found = jnp.dot(
            queries, by_frame[frame][h * DH : (h + 1) * DH, :], preferred_element_type=F32
        )
        scale = lax.rsqrt(jnp.mean(found * found, axis=-1, keepdims=True) + 1e-06)
        return (found * scale).astype(BF)

    for frame in range(2):
        for h in range(HALF):
            mixed_out[frame, :, h * DH : (h + 1) * DH] = attended(frame, h)
    final = remote(
        mixed_out.at[other], mixed_in, near_sems.at[0, 4], near_sems.at[1, 4], {"tm": sibling}
    )
    final.start()
    out_ref[:, pl.ds(base, WIDE)] = mixed_out[c]

    @pl.when(c == parity)
    def _():
        for copy in scatter(block, main_sems):
            copy.wait_send()

    @pl.when(c == last_parity)
    def _():
        for copy in scatter(last_block, last_sems):
            copy.wait_send()

    for copy in gathers:
        copy.wait_send()
    final.wait()
    out_ref[:, pl.ds(pl.multiple_of(other * WIDE, DH), WIDE)] = mixed_in[...]


def run(decay, video, weights, stem):
    dma = pltpu.SemaphoreType.DMA
    vmem = pltpu.VMEM
    return pl.pallas_call(
        kernel,
        out_shape=jax.ShapeDtypeStruct((256, HEADS * DH), BF),
        in_specs=[pl.BlockSpec(memory_space=pltpu.SMEM)]
        + [pl.BlockSpec(memory_space=pltpu.VMEM)] * 3,
        out_specs=pl.BlockSpec(memory_space=pltpu.VMEM),
        scratch_shapes=[
            vmem((2, 112, 1024), BF),
            vmem((16, 1024), BF),
            vmem((8, 128), F32),
            vmem((4, 4, 2, DEPTH, COLS), BF),
            vmem((1152, 1536), BF),
            vmem((576, 1536), BF),
            vmem((512, 1536), BF),
            vmem((512, COLS), BF),
            vmem((2, 8, 128), F32),
            vmem((8, 128), F32),
            vmem((ROW, 2 * SHARE, DH), BF),
            vmem((ROW, 2 * SHARE, DH), BF),
            vmem((SHARE, DH), BF),
            vmem((ZS, SHARE, DH), BF),
            vmem((ZS, 8, 128), F32),
            vmem((2 * SHARE, DH), BF),
            vmem((ROW, 2 * SHARE, DH), BF),
            vmem((2, 256, WIDE), BF),
            vmem((256, WIDE), BF),
            dma((2, 5)),
            dma((2, 2, 4)),
            dma((2, 4)),
            dma((2, 2, 4)),
            dma((2, 4)),
            dma((2, 4, 2, SIDE)),
            dma((2, 4, 2, SIDE, SIDE)),
            dma((2,)),
            dma((2, ROW)),
            dma((2, ZS)),
            dma((2, ZS)),
            dma((2, ROW)),
        ],
        compiler_params=pltpu.CompilerParams(collective_id=0, has_side_effects=True),
        name="frames",
    )(decay, video, weights, stem)


def local(video, stem_weight, w_qkv, decay):
    image = video.reshape(96, 1024)
    stem = stem_weight.reshape(64, 36)
    mixed = run(decay, image, w_qkv, stem)
    return mixed.reshape(1, 2, 128, HEADS * DH)


def solution(mesh):
    return jax.shard_map(
        local,
        mesh=mesh,
        in_specs=(P("tm", None, "row", None), P(), P("tm", None), P("tm", None)),
        out_specs=P("tm", "row", None, None),
        check_vma=False,
    )
```
